256 devices in a mesh: seq: 128 (over y, z_lo, x, core), head: 2 (over z_hi).
Axes of the slice: x: 4, y: 4, z: 8 (z_hi: 2, z_lo: 4; z = z_hi * 4 + z_lo), core: 2. Of those that a mesh axis runs over, the one named last changes fastest.
Arguments:
- queries: bfloat16 [65536, 1024], P('seq', 'head'), may hold values from -8 to 8
- keys: bfloat16 [65536, 1024], P('seq', 'head'), may hold values from -8 to 8
- values: bfloat16 [65536, 1024], P('seq', 'head'), may hold values from -6 to 6
- distances: int32 [4], replicated, may hold values from 1 to 64, as said below
- feature_proj: bfloat16 [64, 128], replicated, may hold values from -6 to 6
- out_proj: bfloat16 [1024, 1024], P('head'), may hold values from -0.1875 to 0.1875
Outputs:
- mixed: bfloat16 [65536, 1024], P('seq', 'head')
The draws below stay inside these ranges and needn't reach their ends.
Inputs may be any that keep to these rules, and one draw needn't show every extreme that they name: `distances`: four different powers of two; 1 and 128 // 2 are always among them.
All inputs are finite; a program needn't handle non-finite values.
Results may differ from the reference program's by a relative error of at most 0.018.
Values may be sent and summed in bfloat16 or wider, within the bound.
A program may use at most 128 MiB of HBM per device.

```python
import jax
import jax.numpy as jnp
from jax import lax

HEADS = 16
HEAD_DIM = 64
FEATURES = 128
PARTNERS = 4
TOK_DEV = 512
SEQ = 65536
N_SEQ = 128


def shared_draw(key, salt):
    width = HEADS * HEAD_DIM
    own_key = jax.random.fold_in(key, salt)
    base = jnp.clip(1.4 * jax.random.normal(own_key, (SEQ, width), jnp.float32), -8.0, 8.0)
    return base.astype(jnp.bfloat16)


def draw_queries(key, part):
    return shared_draw(key, 21)


def draw_keys(key, part):
    return shared_draw(key, 37)


def draw_distances(key, part):
    count = N_SEQ.bit_length() - 1
    middle = jax.random.permutation(jax.random.fold_in(key, 5), count - 2) + 1
    bits = jnp.concatenate([jnp.array([0, count - 1], jnp.int32), middle[:2].astype(jnp.int32)])
    bits = jax.random.permutation(jax.random.fold_in(key, 9), bits)
    return jnp.left_shift(jnp.ones((PARTNERS,), jnp.int32), bits).astype(jnp.int32)


def steps_of(rng, shape, cuts, low, top_value):
    def one(axis_at, shards_of):
        heights = jax.random.uniform(jax.random.fold_in(jax.random.fold_in(rng, 6), axis_at), (shards_of,), jnp.float32, low / len(cuts), top_value / len(cuts))
        return jnp.repeat(jnp.exp(heights), shape[axis_at] // shards_of).reshape((-1,) + (1,) * (len(shape) - axis_at - 1))

    factor_of = one(*cuts[0])
    for cut in cuts[1:]:
        factor_of = factor_of * one(*cut)
    return factor_of


def normal_values(stream_key, shape, spread, most, shards=(), held_as=jnp.bfloat16):
    values = jax.random.normal(stream_key, shape, jnp.float32) * spread
    if len(shards) > 0:
        values = steps_of(stream_key, shape, shards, -0.22, 0.18) * values
    return jnp.clip(values, min=-most, max=most).astype(held_as)


def setup_inputs(seed: int = 0) -> dict:
    streams_of = jax.random.split(jax.random.key(seed), 7)
    queries = draw_queries(jax.random.fold_in(streams_of[6], 71), 0)
    keys = draw_keys(jax.random.fold_in(streams_of[6], 71), 0)
    values = normal_values(streams_of[2], (SEQ, HEADS * HEAD_DIM), 1.0, 6.0, ((0, 128), (1, 2)))
    distances = draw_distances(jax.random.fold_in(streams_of[6], 71), 0)
    feature_proj = normal_values(streams_of[4], (HEAD_DIM, FEATURES), 1.0, 6.0)
    out_proj = normal_values(streams_of[5], (HEADS * HEAD_DIM, HEADS * HEAD_DIM), (HEADS * HEAD_DIM) ** -0.5, 0.1875, ((0, 2),))
    return {"queries": queries, "keys": keys, "values": values, "distances": distances, "feature_proj": feature_proj, "out_proj": out_proj}


def reference(queries, keys, values, distances, feature_proj, out_proj):
    blocks = SEQ // TOK_DEV
    width = HEADS * HEAD_DIM
    q_four = queries.reshape(blocks, TOK_DEV, HEADS, HEAD_DIM)
    k_four = keys.reshape(blocks, TOK_DEV, HEADS, HEAD_DIM)
    v_four = values.reshape(blocks, TOK_DEV, HEADS, HEAD_DIM)
    feat = feature_proj.astype(jnp.float32)
    root_quarter = HEAD_DIM ** -0.25
    root_half = HEAD_DIM ** -0.5

    def key_terms(carry, block):
        k_block, v_block = block
        k_float = k_block.astype(jnp.float32)
        proj = jnp.einsum('thd,dr->thr', k_float, feat)
        square = jnp.sum(k_float * k_float, axis=-1, keepdims=True)
        phi_k = jnp.exp(proj * root_quarter - square * 0.5 * root_half).astype(jnp.bfloat16)
        phi_k = lax.optimization_barrier(phi_k).astype(jnp.float32)
        kv_state = carry[0] + jnp.einsum('thr,the->hre', phi_k, v_block.astype(jnp.float32))
        norm_state = carry[1] + jnp.sum(phi_k, axis=0)
        return (kv_state, norm_state), None

    start = (jnp.zeros((HEADS, FEATURES, HEAD_DIM), jnp.float32), jnp.zeros((HEADS, FEATURES), jnp.float32))
    (kv_state, norm_state), _ = lax.scan(key_terms, start, (k_four, v_four))

    def one_block(index):
        q_float = q_four[index].astype(jnp.float32)
        picks = jnp.concatenate([jnp.reshape(index, (1,)).astype(jnp.int32), jnp.bitwise_xor(index, distances).astype(jnp.int32)])
        k_rows = k_four[picks].reshape(-1, HEADS, HEAD_DIM).astype(jnp.float32)
        v_rows = v_four[picks].reshape(-1, HEADS, HEAD_DIM).astype(jnp.float32)
        scores = jnp.einsum('thd,shd->hts', q_float, k_rows) * root_half
        top = jnp.max(scores, axis=-1, keepdims=True)
        probs = jnp.exp(scores - top)
        weights = lax.optimization_barrier(probs.astype(jnp.bfloat16)).astype(jnp.float32)
        numer = jnp.einsum('hts,shd->htd', weights, v_rows)
        attended = jnp.transpose(numer / jnp.sum(probs, axis=-1)[..., None], (1, 0, 2))
        q_proj = jnp.einsum('thd,dr->thr', q_float, feat) * root_quarter
        phi_q = jnp.exp(q_proj - jnp.max(q_proj, axis=-1, keepdims=True))
        low_numer = jnp.einsum('thr,hre->the', phi_q, kv_state, precision=lax.Precision.HIGHEST)
        low_denom = jnp.einsum('thr,hr->th', phi_q, norm_state, precision=lax.Precision.HIGHEST)
        heads_out = (attended + low_numer / low_denom[..., None]).astype(jnp.bfloat16).reshape(TOK_DEV, width)
        return jnp.dot(heads_out, out_proj, preferred_element_type=jnp.float32).astype(jnp.bfloat16)

    mixed = lax.map(one_block, jnp.arange(blocks, dtype=jnp.int32))
    return mixed.reshape(SEQ, width)
```

```python
import functools
import itertools

import jax
import jax.numpy as jnp
from jax import lax
from jax.experimental import pallas as pl
from jax.experimental.pallas import tpu as pltpu
from jax.sharding import Mesh
from jax.sharding import PartitionSpec as P

AXES = ("seq_0", "seq_1", "seq_2", "seq_3", "head")
SEQ = AXES[:4]
BIT_AXIS = {0: (3, 1), 1: (2, 1), 2: (2, 2), 3: (1, 1), 4: (1, 2), 5: (0, 1), 6: (0, 2)}
MESH = pl.DeviceIdType.MESH
HEAD_DIM = 64
TOK = 512
CH = 4
ROOT_QUARTER = HEAD_DIM ** (-0.25)
SQUARE_SCALE = 0.5 * HEAD_DIM ** (-0.5)
F32 = jnp.float32
BF16 = jnp.bfloat16


def flipped(i, mask):
    if mask == 3:
        return 3 - i
    return i + mask - 2 * mask * lax.rem(lax.div(i, mask), 2)


def nt(a, b):
    return lax.dot_general(a, b, (((1,), (1,)), ((), ())), preferred_element_type=F32)


def nn(a, b):
    return jnp.dot(a, b, preferred_element_type=F32)


def kernel(
    bits, q_hbm, k_hbm, v_hbm, feat2, feat2t, w_hbm, out_ref,
    qbuf, kbuf, vbuf, wbuf, phiq, sbuf, att, hout, own, xsend, xrecv,
    st, rc, s4, rx, s1, ry, s2, rz, full, rhs,
    local_sem, kv_send, kv_recv, r_send, r_recv, x_send, x_recv,
):
    me = [lax.axis_index(a) for a in AXES]

    def peer(axis, mask):
        return tuple(flipped(m, mask) if i == axis else m for i, m in enumerate(me))

    core, xi, hd = me[3], me[2], me[4]
    core_peer, head_peer = peer(3, 1), peer(4, 1)
    fours = {n: [peer(axis, d) for d in (1, 2, 3)] for n, axis in (("x", 2), ("z", 1), ("y", 0))}
    partners = [peer(*BIT_AXIS[b]) for b in bits]

    def cols(c):
        return pl.ds(pl.multiple_of(c * 128, 128), 128)

    def rows(i):
        return pl.ds(pl.multiple_of(i * TOK, TOK), TOK)

    locals_of = []
    for c in range(CH):
        locals_of += [
            pltpu.make_async_copy(k_hbm.at[:, cols(c)], kbuf.at[c, rows(0)], local_sem.at[c]),
            pltpu.make_async_copy(v_hbm.at[:, cols(c)], vbuf.at[c, rows(0)], local_sem.at[4 + c]),
            pltpu.make_async_copy(q_hbm.at[:, cols(c)], qbuf.at[c], local_sem.at[8 + c]),
        ]
    w_copy = pltpu.make_async_copy(w_hbm, wbuf, local_sem.at[12])
    for cp in locals_of:
        cp.start()
    w_copy.start()

    barrier = pltpu.get_barrier_semaphore()
    everyone = [core_peer, head_peer] + fours["x"] + fours["y"] + fours["z"]
    for d in everyone:
        pl.semaphore_signal(barrier, inc=1, device_id=d, device_id_type=MESH)
    pl.semaphore_wait(barrier, len(everyone))

    def kv_copies(i, c):
        return [
            pltpu.make_async_remote_copy(
                src_ref=src.at[:, cols(c)], dst_ref=dst.at[c, rows(i + 1)],
                send_sem=kv_send.at[i, c, n], recv_sem=kv_recv.at[i, c, n],
                device_id=partners[i], device_id_type=MESH,
            )
            for n, (src, dst) in enumerate(((k_hbm, kbuf), (v_hbm, vbuf)))
        ]

    def send_kv(c):
        for i in range(4):
            for cp in kv_copies(i, c):
                cp.start()

    def remote(src, dst, n, device):
        return pltpu.make_async_remote_copy(
            src_ref=src, dst_ref=dst, send_sem=r_send.at[n], recv_sem=r_recv.at[n],
            device_id=device, device_id_type=MESH,
        )

    mine4 = pl.ds(core * 4, 4)
    step_core = [remote(st.at[pl.ds((1 - core) * 4, 4)], rc, 0, core_peer)]
    step_x = [remote(s4.at[flipped(xi, d)], rx.at[d - 1], d, fours["x"][d - 1]) for d in (1, 2, 3)]
    step_y = [remote(s1, ry.at[d - 1], 3 + d, fours["y"][d - 1]) for d in (1, 2, 3)]
    step_z = [remote(s2, rz.at[d - 1], 6 + d, fours["z"][d - 1]) for d in (1, 2, 3)]
    owned = core * 4 + xi
    back_x = [remote(full.at[owned], full.at[owned], 9 + d, fours["x"][d - 1]) for d in (1, 2, 3)]
    back_core = [remote(full.at[mine4], full.at[mine4], 13, core_peer)]

    def go(copies):
        for cp in copies:
            cp.start()

    def arrived(copies):
        for cp in copies:
            cp.wait_recv()

    def summed(first, others):
        total = first.astype(F32)
        for d in range(3):
            total = total + others[d].astype(F32)
        return total.astype(BF16)

    send_kv(0)

    for cp in locals_of:
        cp.wait()
    low = lax.broadcasted_iota(jnp.int32, (128, 128), 1) < HEAD_DIM
    ones = jnp.ones((TOK, 128), BF16)
    head_rows = lax.broadcasted_iota(jnp.int32, (256, 256), 0) < 128
    head_lanes = lax.rem(lax.broadcasted_iota(jnp.int32, (256, 256), 1), 128) < HEAD_DIM
    pick = jnp.where(head_rows == head_lanes, 1.0, 0.0).astype(BF16)

    def state_of(c, z):
        k = kbuf[c, rows(0)]
        kf = k.astype(F32)
        sq = kf * kf
        hi = sq.astype(BF16)
        lo = (sq - hi.astype(F32)).astype(BF16)
        square = nt(pick, jnp.concatenate([hi, lo], axis=1))
        phi = jnp.exp(nt(feat2t[...], k) * ROOT_QUARTER - square * SQUARE_SCALE).astype(BF16)
        both = nn(phi, jnp.concatenate([vbuf[c, rows(0)], ones], axis=1))
        st[2 * c] = jnp.where(low, both[:128, :128], both[:128, 128:]).astype(BF16)
        st[2 * c + 1] = jnp.where(low, both[128:, 128:], both[128:, :128]).astype(BF16)
        return z

    lax.fori_loop(0, CH, state_of, 0)
    go(step_core)

    def features_of(c, z):
        proj = nn(qbuf[c], feat2[...]) * ROOT_QUARTER
        for e in range(2):
            part = proj[:, 128 * e : 128 * (e + 1)]
            top = jnp.max(part, axis=1, keepdims=True)
            phiq[c, :, 128 * e : 128 * (e + 1)] = jnp.exp(part - top).astype(BF16)
        return z

    lax.fori_loop(0, CH, features_of, 0)

    arrived(step_core)
    for i in range(4):
        s4[i] = (st[core * 4 + i].astype(F32) + rc[i].astype(F32)).astype(BF16)
    go(step_x)
    send_kv(1)

    low_tok = lax.broadcasted_iota(jnp.int32, (TOK, 128), 1) < HEAD_DIM

    def attend(c):
        def one_head(e, z):
            q = qbuf[c].astype(F32) * HEAD_DIM ** (-0.5)
            q = jnp.where(low_tok == (e == 0), q, 0.0).astype(BF16)

            def scores(p, top):
                s = nt(q, kbuf[c, rows(p)])
                sbuf[p] = s
                for n in range(4):
                    top = jnp.maximum(top, s[:, 128 * n : 128 * (n + 1)])
                return top

            top = lax.fori_loop(0, 5, scores, jnp.full((TOK, 128), -jnp.inf, F32))
            top = jnp.max(top, axis=1, keepdims=True)

            def weigh(p, acc):
                w = jnp.exp(sbuf[p] - top).astype(BF16)
                return acc + nn(w, jnp.concatenate([vbuf[c, rows(p)], ones], axis=1))

            acc = lax.fori_loop(0, 5, weigh, jnp.zeros((TOK, 256), F32))
            got = acc[:, :128] / acc[:, 128:]
            att[c] = jnp.where(low_tok == (e == 0), got, att[c])
            return z

        lax.fori_loop(0, 2, one_head, 0)

    def chunk(c, z):
        for i in range(4):
            for cp in kv_copies(i, c):
                cp.wait_recv()
        attend(c)

        @pl.when(c == 0)
        def _():
            arrived(step_x)
            s1[...] = summed(s4[xi], rx)
            go(step_y)
            send_kv(2)

        @pl.when(c == 1)
        def _():
            arrived(step_y)
            s2[...] = summed(s1[...], ry)
            go(step_z)
            send_kv(3)

        @pl.when(c == 2)
        def _():
            arrived(step_z)
            full[owned] = summed(s2[...], rz)
            go(back_x)

        return z

    lax.fori_loop(0, CH, chunk, 0)

    arrived(back_x)
    go(back_core)
    w_copy.wait()
    arrived(back_core)

    def right_side(c, z):
        even, odd = full[2 * c].astype(F32), full[2 * c + 1].astype(F32)
        rhs[c, :128, :128] = jnp.where(low, even, 0.0).astype(BF16)
        rhs[c, 128:, :128] = jnp.where(low, 0.0, odd).astype(BF16)
        rhs[c, :128, 128:] = jnp.where(low, pltpu.roll(even, 64, 1), 0.0).astype(BF16)
        rhs[c, 128:, 128:] = jnp.where(low, 0.0, pltpu.roll(odd, 64, 1)).astype(BF16)
        return z

    lax.fori_loop(0, CH, right_side, 0)

    def exchange(t):
        return pltpu.make_async_remote_copy(
            src_ref=xsend.at[t], dst_ref=xrecv.at[t], send_sem=x_send.at[t], recv_sem=x_recv.at[t],
            device_id=head_peer, device_id_type=MESH,
        )

    def project(t, z):
        here = pl.ds(pl.multiple_of(t * 128, 128), 128)
        for c in range(CH):
            both = nn(phiq[c, here, :], rhs[c])
            hout[:, 128 * c : 128 * (c + 1)] = (att[c, here, :] + both[:, :128] / both[:, 128:]).astype(BF16)
        far = pl.ds(pl.multiple_of((1 - hd) * 512, 512), 512)
        near = pl.ds(pl.multiple_of(hd * 512, 512), 512)
        xsend[t] = nn(hout[...], wbuf[:, far]).astype(BF16)
        exchange(t).start()
        own[t] = nn(hout[...], wbuf[:, near])
        return z

    lax.fori_loop(0, 4, project, 0)

    def finish(t, z):
        exchange(t).wait_recv()
        here = pl.ds(pl.multiple_of(t * 128, 128), 128)
        out_ref[here, :] = (own[t] + xrecv[t].astype(F32)).astype(BF16)
        return z

    lax.fori_loop(0, 4, finish, 0)

    for c in range(CH):
        for i in range(4):
            for cp in kv_copies(i, c):
                cp.wait_send()
        exchange(c).wait_send()
    for cp in step_core + step_x + step_y + step_z + back_x + back_core:
        cp.wait_send()


def fused(n, bits, queries, keys, values, feat2, feat2t, out_proj):
    vmem = pl.BlockSpec(memory_space=pltpu.VMEM)
    hbm = pl.BlockSpec(memory_space=pl.ANY)
    dma = pltpu.SemaphoreType.DMA
    state = pltpu.VMEM((128, 128), BF16)
    return pl.pallas_call(
        functools.partial(kernel, bits),
        out_shape=jax.ShapeDtypeStruct((TOK, 512), BF16),
        in_specs=[hbm, hbm, hbm, vmem, vmem, hbm],
        out_specs=vmem,
        scratch_shapes=[
            pltpu.VMEM((CH, TOK, 128), BF16),
            pltpu.VMEM((CH, 5 * TOK, 128), BF16),
            pltpu.VMEM((CH, 5 * TOK, 128), BF16),
            pltpu.VMEM((512, 1024), BF16),
            pltpu.VMEM((CH, TOK, 256), BF16),
            pltpu.VMEM((5, TOK, TOK), F32),
            pltpu.VMEM((CH, TOK, 128), F32),
            pltpu.VMEM((128, 512), BF16),
            pltpu.VMEM((4, 128, 512), F32),
            pltpu.VMEM((4, 128, 512), BF16),
            pltpu.VMEM((4, 128, 512), BF16),
            pltpu.VMEM((8, 128, 128), BF16),
            pltpu.VMEM((4, 128, 128), BF16),
            pltpu.VMEM((4, 128, 128), BF16),
            pltpu.VMEM((3, 128, 128), BF16),
            state,
            pltpu.VMEM((3, 128, 128), BF16),
            state,
            pltpu.VMEM((3, 128, 128), BF16),
            pltpu.VMEM((8, 128, 128), BF16),
            pltpu.VMEM((CH, 256, 256), BF16),
            dma((13,)), dma((4, CH, 2)), dma((4, CH, 2)), dma((14,)), dma((14,)), dma((4,)), dma((4,)),
        ],
        compiler_params=pltpu.CompilerParams(
            collective_id=n, has_side_effects=True, vmem_limit_bytes=48 << 20
        ),
        name="fused_%d_%d" % (bits[1], bits[2]),
    )(queries, keys, values, feat2, feat2t, out_proj)


def per_device(queries, keys, values, distances, feature_proj, out_proj):
    zero = jnp.zeros_like(feature_proj)
    feat2 = jnp.block([[feature_proj, zero], [zero, feature_proj]])
    pairs = list(itertools.combinations(range(1, 6), 2))
    there = [jnp.any(distances == (1 << b)) for b in range(7)]
    index = sum(jnp.where(there[a] & there[b], n, 0) for n, (a, b) in enumerate(pairs))
    branches = [functools.partial(fused, n, (6, a, b, 0)) for n, (a, b) in enumerate(pairs)]
    return lax.switch(index, branches, queries, keys, values, feat2, feat2.T, out_proj)


def solution(mesh):
    split = Mesh(mesh.devices.reshape(4, 4, 4, 2, mesh.shape["head"]), AXES)
    in_specs = (P(SEQ, "head"), P(SEQ, "head"), P(SEQ, "head"), P(), P(), P("head", None))
    return jax.shard_map(
        per_device, mesh=split, in_specs=in_specs, out_specs=P(SEQ, "head"), check_vma=False
    )
```

```python
import functools
import itertools

import jax
import jax.numpy as jnp
from jax import lax
from jax.experimental import pallas as pl
from jax.experimental.pallas import tpu as pltpu
from jax.sharding import Mesh
from jax.sharding import PartitionSpec as P

AXES = ("seq_0", "seq_1", "seq_2", "seq_3", "head")
SEQ = AXES[:4]
BIT_AXIS = {0: (3, 1), 1: (2, 1), 2: (2, 2), 3: (1, 1), 4: (1, 2), 5: (0, 1), 6: (0, 2)}
MESH = pl.DeviceIdType.MESH
HEAD_DIM = 64
TOK = 512
CH = 4
TILE = 128
ROOT_QUARTER = HEAD_DIM ** (-0.25)
SQUARE_SCALE = 0.5 * HEAD_DIM ** (-0.5)
F32 = jnp.float32
BF16 = jnp.bfloat16


def flipped(i, mask):
    if mask == 3:
        return 3 - i
    return i + mask - 2 * mask * lax.rem(lax.div(i, mask), 2)


def nt(a, b):
    return lax.dot_general(a, b, (((1,), (1,)), ((), ())), preferred_element_type=F32)


def nn(a, b):
    return jnp.dot(a, b, preferred_element_type=F32)


def kernel(
    bits, q_hbm, k_hbm, v_hbm, f_hbm, w_hbm, out_ref,
    feat, qbuf, kbuf, vbuf, near, far, feat2, feat2t, phiq, sbuf, tops, sums, att, ho_send, ho_recv, own,
    st, rc, s4, rx, s1, ry, s2, rz, full, rhs,
    local_sem, kv_send, kv_recv, r_send, r_recv, x_send, x_recv,
):
    me = [lax.axis_index(a) for a in AXES]

    def peer(axis, mask):
        return tuple(flipped(m, mask) if i == axis else m for i, m in enumerate(me))

    yi, xi, core, hd = me[0], me[2], me[3], me[4]
    core_peer, head_peer = peer(3, 1), peer(4, 1)
    fours = {n: [peer(axis, d) for d in (1, 2, 3)] for n, axis in (("x", 2), ("z", 1), ("y", 0))}
    partners = [peer(*BIT_AXIS[b]) for b in bits]

    def part(i, size):
        return pl.ds(pl.multiple_of(i * size, size), size)

    def kv_local(c):
        return [
            pltpu.make_async_copy(k_hbm.at[:, part(c, 128)], kbuf.at[c, part(0, TOK)], local_sem.at[c]),
            pltpu.make_async_copy(v_hbm.at[:, part(c, 128)], vbuf.at[c, part(0, TOK)], local_sem.at[4 + c]),
        ]

    def q_local(c):
        return [pltpu.make_async_copy(q_hbm.at[:, part(c, 128)], qbuf.at[c], local_sem.at[8 + c])]

    w_local = [pltpu.make_async_copy(w_hbm.at[:, part(hd, 512)], near, local_sem.at[12])]
    f_local = pltpu.make_async_copy(f_hbm, feat, local_sem.at[13])

    def go(copies):
        for cp in copies:
            cp.start()

    def arrived(copies):
        for cp in copies:
            cp.wait_recv()

    barrier = pltpu.get_barrier_semaphore()
    everyone = [core_peer, head_peer] + fours["x"] + fours["y"] + fours["z"]
    for d in everyone:
        pl.semaphore_signal(barrier, inc=1, device_id=d, device_id_type=MESH)

    f_local.start()
    def load(c, z):
        go(kv_local(c) + q_local(c))
        return z

    lax.fori_loop(0, CH, load, 0)
    go(w_local)
    f_local.wait()
    f = feat[...].astype(F32)
    nil = jnp.zeros_like(f)
    block = jnp.concatenate([jnp.concatenate([f, nil], axis=1), jnp.concatenate([nil, f], axis=1)], axis=0)
    feat2[...] = block.astype(BF16)
    feat2t[...] = block.T.astype(BF16)

    pl.semaphore_wait(barrier, len(everyone))

    def kv_copies(i, c):
        return [
            pltpu.make_async_remote_copy(
                src_ref=src.at[:, part(c, 128)], dst_ref=dst.at[c, part(i + 1, TOK)],
                send_sem=kv_send.at[i, c, n], recv_sem=kv_recv.at[i, c, n],
                device_id=partners[i], device_id_type=MESH,
            )
            for n, (src, dst) in enumerate(((k_hbm, kbuf), (v_hbm, vbuf)))
        ]

    def send_kv(c):
        for i in range(4):
            go(kv_copies(i, c))

    def remote(src, dst, n, device):
        return pltpu.make_async_remote_copy(
            src_ref=src, dst_ref=dst, send_sem=r_send.at[n], recv_sem=r_recv.at[n],
            device_id=device, device_id_type=MESH,
        )

    mine4 = pl.ds(core * 4, 4)
    owned = core * 4 + xi
    step_core = [remote(st.at[pl.ds((1 - core) * 4, 4)], rc, 0, core_peer)]
    step_x = [remote(s4.at[flipped(xi, d)], rx.at[d - 1], d, fours["x"][d - 1]) for d in (1, 2, 3)]
    step_y = [remote(s1, ry.at[d - 1], 3 + d, fours["y"][d - 1]) for d in (1, 2, 3)]
    step_z = [remote(s2, rz.at[d - 1], 6 + d, fours["z"][d - 1]) for d in (1, 2, 3)]
    back_x = [remote(full.at[owned], full.at[owned], 9 + d, fours["x"][d - 1]) for d in (1, 2, 3)]
    back_core = [remote(full.at[mine4], full.at[mine4], 13, core_peer)]
    line = part(core * 16 + yi * 4 + xi, 16)
    four = part(core * 4 + yi, 64)
    half = part(core, 256)
    w_head = [remote(w_hbm.at[line, part(1 - hd, 512)], far.at[line], 14, head_peer)]
    w_x = [remote(far.at[line], far.at[line], 14 + d, fours["x"][d - 1]) for d in (1, 2, 3)]
    w_y = [remote(far.at[four], far.at[four], 17 + d, fours["y"][d - 1]) for d in (1, 2, 3)]
    w_core = [remote(far.at[half], far.at[half], 21, core_peer)]

    def summed(first, others):
        total = first.astype(F32)
        for d in range(3):
            total = total + others[d].astype(F32)
        return total.astype(BF16)

    go(w_head)
    send_kv(0)

    low = lax.broadcasted_iota(jnp.int32, (128, 128), 1) < HEAD_DIM
    ones = jnp.ones((TOK, 128), BF16)
    head_rows = lax.broadcasted_iota(jnp.int32, (16, 256), 0) < 8
    head_lanes = lax.rem(lax.broadcasted_iota(jnp.int32, (16, 256), 1), 128) < HEAD_DIM
    pick = jnp.where(head_rows == head_lanes, 1.0, 0.0).astype(BF16)

    def state_of(c, z):
        for cp in kv_local(c):
            cp.wait()
        k = kbuf[c, part(0, TOK)]
        kf = k.astype(F32)
        sq = kf * kf
        hi = sq.astype(BF16)
        lo = (sq - hi.astype(F32)).astype(BF16)
        square = nt(pick, jnp.concatenate([hi, lo], axis=1)) * SQUARE_SCALE
        proj = nt(feat2t[...], k) * ROOT_QUARTER
        phi = jnp.exp(jnp.concatenate([proj[:128] - square[:1], proj[128:] - square[8:9]], axis=0))
        both = nn(phi.astype(BF16), jnp.concatenate([vbuf[c, part(0, TOK)], ones], axis=1))
        st[2 * c] = jnp.where(low, both[:128, :128], both[:128, 128:]).astype(BF16)
        st[2 * c + 1] = jnp.where(low, both[128:, 128:], both[128:, :128]).astype(BF16)
        return z

    lax.fori_loop(0, CH, state_of, 0)
    go(step_core)

    def features_of(c, z):
        q_local(c)[0].wait()

        def rows_of_c(t, z):
            proj = nn(qbuf[c, part(t, TILE), :], feat2[...]) * ROOT_QUARTER
            for e in range(2):
                one = proj[:, 128 * e : 128 * (e + 1)]
                top = jnp.max(one, axis=1, keepdims=True)
                phiq[c, part(t, TILE), 128 * e : 128 * (e + 1)] = jnp.exp(one - top).astype(BF16)
            return z

        return lax.fori_loop(0, 4, rows_of_c, z)

    arrived(step_core)

    def add_core(i, z):
        s4[i] = (st[core * 4 + i].astype(F32) + rc[i].astype(F32)).astype(BF16)
        return z

    lax.fori_loop(0, 4, add_core, 0)
    go(step_x)
    send_kv(1)

    lax.fori_loop(0, CH, features_of, 0)

    arrived(step_x)
    s1[...] = summed(s4[xi], rx)
    go(step_y)
    arrived(w_head)
    go(w_x)

    low_tok = lax.broadcasted_iota(jnp.int32, (TOK, 128), 1) < HEAD_DIM

    def score(c):
        q = qbuf[c].astype(F32) * HEAD_DIM ** (-0.5)
        q = jnp.concatenate([jnp.where(low_tok, q, 0.0), jnp.where(low_tok, 0.0, q)], axis=0).astype(BF16)
        tops[...] = jnp.full((2 * TOK, 128), -jnp.inf, F32)

        def block(p, z):
            s = nt(q, kbuf[c, part(p, TOK)])
            sbuf[p] = s
            top = tops[...]
            for n in range(4):
                top = jnp.maximum(top, s[:, 128 * n : 128 * (n + 1)])
            tops[...] = top
            return z

        lax.fori_loop(0, 5, block, 0)

    def weigh(c):
        tops[...] = jnp.broadcast_to(jnp.max(tops[...], axis=1, keepdims=True), (2 * TOK, 128))
        sums[...] = jnp.zeros((2 * TOK, 256), F32)

        def block(p, z):
            top = tops[...]
            w = [jnp.exp(sbuf[p, :, 128 * n : 128 * (n + 1)] - top).astype(BF16) for n in range(4)]
            rights = jnp.concatenate([vbuf[c, part(p, TOK)], ones], axis=1)
            sums[...] += nn(jnp.concatenate(w, axis=1), rights)
            return z

        lax.fori_loop(0, 5, block, 0)
        got = sums[:, :128] / sums[:, 128:]
        att[c] = jnp.where(low_tok, got[:TOK], got[TOK:])

    def right_side(c, z):
        even, odd = full[2 * c].astype(F32), full[2 * c + 1].astype(F32)
        rhs[c, :128, :128] = jnp.where(low, even, 0.0).astype(BF16)
        rhs[c, 128:, :128] = jnp.where(low, 0.0, odd).astype(BF16)
        rhs[c, :128, 128:] = jnp.where(low, pltpu.roll(even, 64, 1), 0.0).astype(BF16)
        rhs[c, 128:, 128:] = jnp.where(low, 0.0, pltpu.roll(odd, 64, 1)).astype(BF16)
        return z

    def exchange(n):
        c, t = lax.div(n, 4), lax.rem(n, 4)
        return pltpu.make_async_remote_copy(
            src_ref=ho_send.at[c, part(t, TILE)], dst_ref=ho_recv.at[c, part(t, TILE)],
            send_sem=x_send.at[n], recv_sem=x_recv.at[n], device_id=head_peer, device_id_type=MESH,
        )

    def finalize(n, z):
        c, here = lax.div(n, 4), part(lax.rem(n, 4), TILE)
        both = nn(phiq[c, here, :], rhs[c])
        ho_send[c, here, :] = (att[c, here, :] + both[:, :128] / both[:, 128:]).astype(BF16)
        exchange(n).start()
        return z

    def chunk(c, z):
        for n in range(4):
            arrived(kv_copies(n, c))
        score(c)

        @pl.when(c == 0)
        def _():
            arrived(step_y)
            s2[...] = summed(s1[...], ry)
            go(step_z)
            arrived(w_x)
            go(w_y)

        @pl.when(c == 1)
        def _():
            arrived(back_x)
            go(back_core)
            arrived(w_y)
            go(w_core)

        @pl.when(c < 2)
        def _():
            send_kv(c + 2)

        weigh(c)

        @pl.when(c == 0)
        def _():
            arrived(step_z)
            full[owned] = summed(s2[...], rz)
            go(back_x)

        @pl.when(c == 1)
        def _():
            arrived(back_core)
            lax.fori_loop(0, CH, right_side, 0)

        first = jnp.where(c == 1, 0, 4 * c)
        last = jnp.where(c == 0, 0, 4 * c + 4)
        lax.fori_loop(first, last, finalize, 0)
        return z

    lax.fori_loop(0, CH, chunk, 0)

    w_local[0].wait()
    arrived(w_core)

    def rows_of(t):
        return part(t, TILE)

    def first_sum(t, z):
        own[rows_of(t), :] = sum(nn(ho_send[c, rows_of(t), :], near[128 * c : 128 * (c + 1), :]) for c in range(CH))
        return z

    def next_sum(t, z):
        for c in range(3):
            exchange(4 * c + t).wait_recv()
        own[rows_of(t), :] += sum(nn(ho_recv[c, rows_of(t), :], far[128 * c : 128 * (c + 1), :]) for c in range(3))
        return z

    def last_sum(t, z):
        exchange(12 + t).wait_recv()
        out_ref[rows_of(t), :] = (own[rows_of(t), :] + nn(ho_recv[3, rows_of(t), :], far[384:, :])).astype(BF16)
        return z

    lax.fori_loop(0, 4, first_sum, 0)
    lax.fori_loop(0, 4, next_sum, 0)
    lax.fori_loop(0, 4, last_sum, 0)

    def drain(c, z):
        for i in range(4):
            for cp in kv_copies(i, c):
                cp.wait_send()
        for t in range(4):
            exchange(4 * c + t).wait_send()
        return z

    lax.fori_loop(0, CH, drain, 0)
    for cp in step_core + step_x + step_y + step_z + back_x + back_core + w_head + w_x + w_y + w_core:
        cp.wait_send()


def fused(n, bits, queries, keys, values, features, out_proj):
    vmem = pl.BlockSpec(memory_space=pltpu.VMEM)
    hbm = pl.BlockSpec(memory_space=pl.ANY)
    dma = pltpu.SemaphoreType.DMA
    state = pltpu.VMEM((128, 128), BF16)
    three = pltpu.VMEM((3, 128, 128), BF16)
    four = pltpu.VMEM((4, 128, 128), BF16)
    eight = pltpu.VMEM((8, 128, 128), BF16)
    return pl.pallas_call(
        functools.partial(kernel, bits),
        out_shape=jax.ShapeDtypeStruct((TOK, 512), BF16),
        in_specs=[hbm] * 5,
        out_specs=vmem,
        scratch_shapes=[
            pltpu.VMEM((HEAD_DIM, 128), BF16),
            pltpu.VMEM((CH, TOK, 128), BF16),
            pltpu.VMEM((CH, 5 * TOK, 128), BF16),
            pltpu.VMEM((CH, 5 * TOK, 128), BF16),
            pltpu.VMEM((512, 512), BF16),
            pltpu.VMEM((512, 512), BF16),
            pltpu.VMEM((128, 256), BF16),
            pltpu.VMEM((256, 128), BF16),
            pltpu.VMEM((CH, TOK, 256), BF16),
            pltpu.VMEM((5, 2 * TOK, TOK), F32),
            pltpu.VMEM((2 * TOK, 128), F32),
            pltpu.VMEM((2 * TOK, 256), F32),
            pltpu.VMEM((CH, TOK, 128), F32),
            pltpu.VMEM((CH, TOK, 128), BF16),
            pltpu.VMEM((CH, TOK, 128), BF16),
            pltpu.VMEM((TOK, 512), F32),
            eight, four, four, three, state, three, state, three, eight,
            pltpu.VMEM((CH, 256, 256), BF16),
            dma((14,)), dma((4, CH, 2)), dma((4, CH, 2)), dma((22,)), dma((22,)), dma((16,)), dma((16,)),
        ],
        compiler_params=pltpu.CompilerParams(
            collective_id=n, has_side_effects=True, vmem_limit_bytes=48 << 20
        ),
        name="fused_%d_%d" % (bits[1], bits[2]),
    )(queries, keys, values, features, out_proj)


CODE = {1: 0, 2: 1, 3: 2, 4: 4, 5: 7}


def per_device(queries, keys, values, distances, feature_proj, out_proj):
    codes = sum(jnp.where(distances == (1 << b), n, 0) for b, n in CODE.items())
    index = jnp.sum(codes) - 1
    branches = [lambda q, k, v, f, w: jnp.zeros_like(q)] * 11
    for n, (a, b) in enumerate(itertools.combinations(CODE, 2)):
        branches[CODE[a] + CODE[b] - 1] = functools.partial(fused, n, (6, a, b, 0))
    return lax.switch(index, branches, queries, keys, values, feature_proj, out_proj)


def solution(mesh):
    split = Mesh(mesh.devices.reshape(4, 4, 4, 2, mesh.shape["head"]), AXES)
    in_specs = (P(SEQ, "head"), P(SEQ, "head"), P(SEQ, "head"), P(), P(), P("head", None))
    return jax.shard_map(
        per_device, mesh=split, in_specs=in_specs, out_specs=P(SEQ, "head"), check_vma=False
    )
```

```python
import functools
import itertools

import jax
import jax.numpy as jnp
from jax import lax
from jax.experimental import pallas as pl
from jax.experimental.pallas import tpu as pltpu
from jax.sharding import Mesh
from jax.sharding import PartitionSpec as P

AXES = ("seq_0", "seq_1", "seq_2", "seq_3", "head")
SEQ = AXES[:4]
BIT_AXIS = {0: (3, 1), 1: (2, 1), 2: (2, 2), 3: (1, 1), 4: (1, 2), 5: (0, 1), 6: (0, 2)}
MESH = pl.DeviceIdType.MESH
HEAD_DIM = 64
TOK = 512
CH = 4
TILE = 128
ROOT_QUARTER = HEAD_DIM ** (-0.25)
SQUARE_SCALE = 0.5 * HEAD_DIM ** (-0.5)
F32 = jnp.float32
BF16 = jnp.bfloat16


def flipped(i, mask):
    if mask == 3:
        return 3 - i
    return i + mask - 2 * mask * lax.rem(lax.div(i, mask), 2)


def nt(a, b):
    return lax.dot_general(a, b, (((1,), (1,)), ((), ())), preferred_element_type=F32)


def nn(a, b):
    return jnp.dot(a, b, preferred_element_type=F32)


def kernel(
    bits, q_hbm, k_hbm, v_hbm, f_hbm, w_hbm, out_ref,
    feat, qbuf, kbuf, vbuf, near, far, feat2, feat2t, phiq, sbuf, tops, sums, att, ho_send, ho_recv, own,
    st, rc, s4, rx, s1, ry, s2, rz, full, rhs,
    local_sem, kv_send, kv_recv, r_send, r_recv, x_send, x_recv,
):
    me = [lax.axis_index(a) for a in AXES]

    def peer(axis, mask):
        return tuple(flipped(m, mask) if i == axis else m for i, m in enumerate(me))

    yi, xi, core, hd = me[0], me[2], me[3], me[4]
    core_peer, head_peer = peer(3, 1), peer(4, 1)
    fours = {n: [peer(axis, d) for d in (1, 2, 3)] for n, axis in (("x", 2), ("z", 1), ("y", 0))}
    partners = [peer(*BIT_AXIS[b]) for b in bits]

    def part(i, size):
        return pl.ds(pl.multiple_of(i * size, size), size)

    def kv_local(c):
        return [
            pltpu.make_async_copy(k_hbm.at[:, part(c, 128)], kbuf.at[c, part(0, TOK)], local_sem.at[c]),
            pltpu.make_async_copy(v_hbm.at[:, part(c, 128)], vbuf.at[c, part(0, TOK)], local_sem.at[4 + c]),
        ]

    def q_local(c):
        return [pltpu.make_async_copy(q_hbm.at[:, part(c, 128)], qbuf.at[c], local_sem.at[8 + c])]

    w_local = [pltpu.make_async_copy(w_hbm.at[:, part(hd, 512)], near, local_sem.at[12])]
    f_local = pltpu.make_async_copy(f_hbm, feat, local_sem.at[13])

    def go(copies):
        for cp in copies:
            cp.start()

    def arrived(copies):
        for cp in copies:
            cp.wait_recv()

    barrier = pltpu.get_barrier_semaphore()
    everyone = [core_peer, head_peer] + fours["x"] + fours["y"] + fours["z"]
    for d in everyone:
        pl.semaphore_signal(barrier, inc=1, device_id=d, device_id_type=MESH)

    f_local.start()
    def load(c, z):
        go(kv_local(c) + q_local(c))
        return z

    lax.fori_loop(0, CH, load, 0)
    go(w_local)
    f_local.wait()
    f = feat[...].astype(F32)
    nil = jnp.zeros_like(f)
    block = jnp.concatenate([jnp.concatenate([f, nil], axis=1), jnp.concatenate([nil, f], axis=1)], axis=0)
    feat2[...] = block.astype(BF16)
    feat2t[...] = block.T.astype(BF16)

    pl.semaphore_wait(barrier, len(everyone))

    def kv_copies(i, c):
        return [
            pltpu.make_async_remote_copy(
                src_ref=src.at[:, part(c, 128)], dst_ref=dst.at[c, part(i + 1, TOK)],
                send_sem=kv_send.at[i, c, n], recv_sem=kv_recv.at[i, c, n],
                device_id=partners[i], device_id_type=MESH,
            )
            for n, (src, dst) in enumerate(((k_hbm, kbuf), (v_hbm, vbuf)))
        ]

    def send_kv(c):
        for i in range(4):
            go(kv_copies(i, c))

    def remote(src, dst, n, device):
        return pltpu.make_async_remote_copy(
            src_ref=src, dst_ref=dst, send_sem=r_send.at[n], recv_sem=r_recv.at[n],
            device_id=device, device_id_type=MESH,
        )

    mine4 = pl.ds(core * 4, 4)
    owned = core * 4 + xi
    step_core = [remote(st.at[pl.ds((1 - core) * 4, 4)], rc, 0, core_peer)]
    step_x = [remote(s4.at[flipped(xi, d)], rx.at[d - 1], d, fours["x"][d - 1]) for d in (1, 2, 3)]
    step_y = [remote(s1, ry.at[d - 1], 3 + d, fours["y"][d - 1]) for d in (1, 2, 3)]
    step_z = [remote(s2, rz.at[d - 1], 6 + d, fours["z"][d - 1]) for d in (1, 2, 3)]
    back_x = [remote(full.at[owned], full.at[owned], 9 + d, fours["x"][d - 1]) for d in (1, 2, 3)]
    back_core = [remote(full.at[mine4], full.at[mine4], 13, core_peer)]
    line = part(core * 16 + yi * 4 + xi, 16)
    four = part(core * 4 + yi, 64)
    half = part(core, 256)
    w_head = [remote(w_hbm.at[line, part(1 - hd, 512)], far.at[line], 14, head_peer)]
    w_x = [remote(far.at[line], far.at[line], 14 + d, fours["x"][d - 1]) for d in (1, 2, 3)]
    w_y = [remote(far.at[four], far.at[four], 17 + d, fours["y"][d - 1]) for d in (1, 2, 3)]
    w_core = [remote(far.at[half], far.at[half], 21, core_peer)]

    def summed(first, others):
        total = first.astype(F32)
        for d in range(3):
            total = total + others[d].astype(F32)
        return total.astype(BF16)

    go(w_head)
    send_kv(0)

    low = lax.broadcasted_iota(jnp.int32, (128, 128), 1) < HEAD_DIM
    ones = jnp.ones((TOK, 128), BF16)
    head_rows = lax.broadcasted_iota(jnp.int32, (16, 256), 0) < 8
    head_lanes = lax.rem(lax.broadcasted_iota(jnp.int32, (16, 256), 1), 128) < HEAD_DIM
    pick = jnp.where(head_rows == head_lanes, 1.0, 0.0).astype(BF16)

    def state_of(c, z):
        for cp in kv_local(c):
            cp.wait()
        k = kbuf[c, part(0, TOK)]
        kf = k.astype(F32)
        sq = kf * kf
        hi = sq.astype(BF16)
        lo = (sq - hi.astype(F32)).astype(BF16)
        square = nt(pick, jnp.concatenate([hi, lo], axis=1)) * SQUARE_SCALE
        proj = nt(feat2t[...], k) * ROOT_QUARTER
        phi = jnp.exp(jnp.concatenate([proj[:128] - square[:1], proj[128:] - square[8:9]], axis=0))
        both = nn(phi.astype(BF16), jnp.concatenate([vbuf[c, part(0, TOK)], ones], axis=1))
        st[2 * c] = jnp.where(low, both[:128, :128], both[:128, 128:]).astype(BF16)
        st[2 * c + 1] = jnp.where(low, both[128:, 128:], both[128:, :128]).astype(BF16)
        return z

    lax.fori_loop(0, CH, state_of, 0)
    go(step_core)

    def features_of(c, z):
        q_local(c)[0].wait()

        def rows_of_c(t, z):
            proj = nn(qbuf[c, part(t, TILE), :], feat2[...]) * ROOT_QUARTER
            for e in range(2):
                one = proj[:, 128 * e : 128 * (e + 1)]
                top = jnp.max(one, axis=1, keepdims=True)
                phiq[c, part(t, TILE), 128 * e : 128 * (e + 1)] = jnp.exp(one - top).astype(BF16)
            return z

        return lax.fori_loop(0, 4, rows_of_c, z)

    arrived(step_core)

    def add_core(i, z):
        s4[i] = (st[core * 4 + i].astype(F32) + rc[i].astype(F32)).astype(BF16)
        return z

    lax.fori_loop(0, 4, add_core, 0)
    go(step_x)
    send_kv(1)

    lax.fori_loop(0, CH, features_of, 0)

    arrived(step_x)
    s1[...] = summed(s4[xi], rx)
    go(step_y)
    arrived(w_head)
    go(w_x)

    low_tok = lax.broadcasted_iota(jnp.int32, (TOK, 128), 1) < HEAD_DIM

    def score(c):
        q = qbuf[c].astype(F32) * HEAD_DIM ** (-0.5)
        q = jnp.concatenate([jnp.where(low_tok, q, 0.0), jnp.where(low_tok, 0.0, q)], axis=0).astype(BF16)
        tops[...] = jnp.full((2 * TOK, 128), -jnp.inf, F32)

        def block(p, z):
            s = nt(q, kbuf[c, part(p, TOK)])
            sbuf[p] = s
            top = tops[...]
            for n in range(4):
                top = jnp.maximum(top, s[:, 128 * n : 128 * (n + 1)])
            tops[...] = top
            return z

        lax.fori_loop(0, 5, block, 0)

    def weigh(c):
        tops[...] = jnp.broadcast_to(jnp.max(tops[...], axis=1, keepdims=True), (2 * TOK, 128))
        sums[...] = jnp.zeros((2 * TOK, 256), F32)

        def block(p, z):
            top = tops[...]
            w = [jnp.exp(sbuf[p, :, 128 * n : 128 * (n + 1)] - top).astype(BF16) for n in range(4)]
            rights = jnp.concatenate([vbuf[c, part(p, TOK)], ones], axis=1)
            sums[...] += nn(jnp.concatenate(w, axis=1), rights)
            return z

        lax.fori_loop(0, 5, block, 0)
        got = sums[:, :128] / sums[:, 128:]
        att[c] = jnp.where(low_tok, got[:TOK], got[TOK:])

    def right_side(c, z):
        even, odd = full[2 * c].astype(F32), full[2 * c + 1].astype(F32)
        rhs[c, :128, :128] = jnp.where(low, even, 0.0).astype(BF16)
        rhs[c, 128:, :128] = jnp.where(low, 0.0, odd).astype(BF16)
        rhs[c, :128, 128:] = jnp.where(low, pltpu.roll(even, 64, 1), 0.0).astype(BF16)
        rhs[c, 128:, 128:] = jnp.where(low, 0.0, pltpu.roll(odd, 64, 1)).astype(BF16)
        return z

    def exchange(n):
        c, t = lax.div(n, 4), lax.rem(n, 4)
        return pltpu.make_async_remote_copy(
            src_ref=ho_send.at[c, part(t, TILE)], dst_ref=ho_recv.at[c, part(t, TILE)],
            send_sem=x_send.at[n], recv_sem=x_recv.at[n], device_id=head_peer, device_id_type=MESH,
        )

    def finalize(n, z):
        c, here = lax.div(n, 4), part(lax.rem(n, 4), TILE)
        both = nn(phiq[c, here, :], rhs[c])
        ho_send[c, here, :] = (att[c, here, :] + both[:, :128] / both[:, 128:]).astype(BF16)
        exchange(n).start()
        return z

    def chunk(c, z):
        for n in range(4):
            arrived(kv_copies(n, c))
        score(c)

        @pl.when(c == 0)
        def _():
            arrived(step_y)
            s2[...] = summed(s1[...], ry)
            go(step_z)
            arrived(w_x)
            go(w_y)

        @pl.when(c == 1)
        def _():
            arrived(back_x)
            go(back_core)
            arrived(w_y)
            go(w_core)

        @pl.when(c < 2)
        def _():
            send_kv(c + 2)

        weigh(c)

        @pl.when(c == 0)
        def _():
            arrived(step_z)
            full[owned] = summed(s2[...], rz)
            go(back_x)

        @pl.when(c == 1)
        def _():
            arrived(back_core)
            lax.fori_loop(0, CH, right_side, 0)

        first = jnp.where(c == 1, 0, 4 * c)
        last = jnp.where(c == 0, 0, 4 * c + 4)
        lax.fori_loop(first, last, finalize, 0)
        return z

    lax.fori_loop(0, CH, chunk, 0)

    w_local[0].wait()
    arrived(w_core)

    def rows_of(t):
        return part(t, TILE)

    def first_sum(t, z):
        own[rows_of(t), :] = sum(nn(ho_send[c, rows_of(t), :], near[128 * c : 128 * (c + 1), :]) for c in range(CH))
        return z

    def next_sum(t, z):
        for c in range(3):
            exchange(4 * c + t).wait_recv()
        own[rows_of(t), :] += sum(nn(ho_recv[c, rows_of(t), :], far[128 * c : 128 * (c + 1), :]) for c in range(3))
        return z

    def last_sum(t, z):
        exchange(12 + t).wait_recv()
        out_ref[rows_of(t), :] = (own[rows_of(t), :] + nn(ho_recv[3, rows_of(t), :], far[384:, :])).astype(BF16)
        return z

    lax.fori_loop(0, 4, first_sum, 0)
    lax.fori_loop(0, 4, next_sum, 0)
    lax.fori_loop(0, 4, last_sum, 0)

    def drain(c, z):
        for i in range(4):
            for cp in kv_copies(i, c):
                cp.wait_send()
        for t in range(4):
            exchange(4 * c + t).wait_send()
        return z

    lax.fori_loop(0, CH, drain, 0)
    for cp in step_core + step_x + step_y + step_z + back_x + back_core + w_head + w_x + w_y + w_core:
        cp.wait_send()


def fused(n, bits, queries, keys, values, features, out_proj):
    vmem = pl.BlockSpec(memory_space=pltpu.VMEM)
    hbm = pl.BlockSpec(memory_space=pl.ANY)
    dma = pltpu.SemaphoreType.DMA
    state = pltpu.VMEM((128, 128), BF16)
    three = pltpu.VMEM((3, 128, 128), BF16)
    four = pltpu.VMEM((4, 128, 128), BF16)
    eight = pltpu.VMEM((8, 128, 128), BF16)
    return pl.pallas_call(
        functools.partial(kernel, bits),
        out_shape=jax.ShapeDtypeStruct((TOK, 512), BF16),
        in_specs=[hbm] * 5,
        out_specs=vmem,
        scratch_shapes=[
            pltpu.VMEM((HEAD_DIM, 128), BF16),
            pltpu.VMEM((CH, TOK, 128), BF16),
            pltpu.VMEM((CH, 5 * TOK, 128), BF16),
            pltpu.VMEM((CH, 5 * TOK, 128), BF16),
            pltpu.VMEM((512, 512), BF16),
            pltpu.VMEM((512, 512), BF16),
            pltpu.VMEM((128, 256), BF16),
            pltpu.VMEM((256, 128), BF16),
            pltpu.VMEM((CH, TOK, 256), BF16),
            pltpu.VMEM((5, 2 * TOK, TOK), F32),
            pltpu.VMEM((2 * TOK, 128), F32),
            pltpu.VMEM((2 * TOK, 256), F32),
            pltpu.VMEM((CH, TOK, 128), F32),
            pltpu.VMEM((CH, TOK, 128), BF16),
            pltpu.VMEM((CH, TOK, 128), BF16),
            pltpu.VMEM((TOK, 512), F32),
            eight, four, four, three, state, three, state, three, eight,
            pltpu.VMEM((CH, 256, 256), BF16),
            dma((14,)), dma((4, CH, 2)), dma((4, CH, 2)), dma((22,)), dma((22,)), dma((16,)), dma((16,)),
        ],
        compiler_params=pltpu.CompilerParams(
            collective_id=n, has_side_effects=True, vmem_limit_bytes=48 << 20
        ),
        name="fused_%d_%d" % (bits[1], bits[2]),
    )(queries, keys, values, features, out_proj)


CODE = {1: 0, 2: 1, 3: 2, 4: 4, 5: 7}


def per_device(queries, keys, values, distances, feature_proj, out_proj):
    codes = sum(jnp.where(distances == (1 << b), n, 0) for b, n in CODE.items())
    index = jnp.sum(codes) - 1
    branches = [lambda q, k, v, f, w: jnp.zeros_like(q)] * 11
    for n, (a, b) in enumerate(itertools.combinations(CODE, 2)):
        branches[CODE[a] + CODE[b] - 1] = functools.partial(fused, n, (6, a, b, 0))
    operands = (queries, keys, values, feature_proj, out_proj)
    return lax.cond(
        index < 5,
        lambda *a: lax.switch(index, branches[:5], *a),
        lambda *a: lax.switch(index - 5, branches[5:], *a),
        *operands,
    )


def solution(mesh):
    split = Mesh(mesh.devices.reshape(4, 4, 4, 2, mesh.shape["head"]), AXES)
    in_specs = (P(SEQ, "head"), P(SEQ, "head"), P(SEQ, "head"), P(), P(), P("head", None))
    return jax.shard_map(
        per_device, mesh=split, in_specs=in_specs, out_specs=P(SEQ, "head"), check_vma=False
    )
```
